32 devices in a mesh: dp: 4 (over y, core), seq: 8 (over z, x).
Axes of the slice: x: 2, y: 2, z: 4, core: 2. Of those that a mesh axis runs over, the one named last changes fastest.
Arguments:
- query: bfloat16 [8, 2048, 32, 128], P('dp', 'seq'), may hold values from -128 to 128
- keys: bfloat16 [8, 2048, 4, 128], P('dp', 'seq'), may hold values from -4.5 to 4.5
- values: bfloat16 [8, 2048, 4, 128], P('dp', 'seq'), may hold values from -6 to 6
- output: bfloat16 [8, 2048, 32, 128], P('dp', 'seq'), may hold values from -6 to 6
- out_grad: bfloat16 [8, 2048, 32, 128], P('dp', 'seq'), may hold values from -6 to 6
- lengths: int32 [8], P('dp'), may hold values from 341 to 2048, as said below
- margins: float32 [4], P('dp'), may hold values from -3 to 3
Outputs:
- query_grad: bfloat16 [8, 2048, 32, 128], P('dp', 'seq')
- key_grad: bfloat16 [8, 2048, 4, 128], P('dp', 'seq')
- value_grad: bfloat16 [8, 2048, 4, 128], P('dp', 'seq')
The draws below stay inside these ranges and needn't reach their ends.
Inputs may be any that keep to these rules, and one draw needn't show every extreme that they name: `lengths`: sequence 2p is pair p's chosen response and 2p + 1 its rejected one; some sequence has exactly 2048 tokens.
All inputs are finite; a program needn't handle non-finite values.
Results may differ from the reference program's by a relative error of at most 0.009.
Values may be sent and summed in bfloat16 or wider, within the bound.
A program may use at most 128 MiB of HBM per device.

```python
import math
import jax
import jax.numpy as jnp
from jax import lax

HEADS = 32
KV_HEADS = 4
HEAD_DIM = 128
MAX_LEN = 2048
PAIRS_DEV = 1
PAIRS = 4
SEQS = 8
N_DP = 4


def key_base(key):
    base = jax.random.normal(jax.random.fold_in(key, 11), (SEQS, MAX_LEN, KV_HEADS, HEAD_DIM), jnp.float32)
    return jnp.clip(base, -4.5, 4.5)


def draw_keys(key, part):
    base = key_base(key)
    return base.astype(jnp.bfloat16)


def draw_query(key, part):
    fresh = jax.random.normal(jax.random.fold_in(key, 12), (SEQS, MAX_LEN, HEADS, HEAD_DIM), jnp.float32)
    fresh = jnp.clip(fresh, -4.5, 4.5)
    return fresh.astype(jnp.bfloat16)


def draw_lengths(key, part):
    index = jnp.arange(SEQS)
    group = index // (2 * PAIRS_DEV)
    third = MAX_LEN // 3
    upper = third + (MAX_LEN - third) * group // max(N_DP - 1, 1)
    lower = upper // 2
    raw = jax.random.randint(key, (SEQS,), 0, 1048576)
    length = lower + raw % (upper - lower + 1)
    length = jnp.where(index == (N_DP - 1) * 2 * PAIRS_DEV, MAX_LEN, length)
    length = jnp.where(index == 2 * PAIRS_DEV - 1, third // 2, length)
    return length.astype(jnp.int32)


def block_levels(rng, shape, shards, smallest, top_value):
    factor_of, own = 1.0, jax.random.fold_in(rng, 6)
    for dim, blocks in shards:
        steps = jnp.exp(jax.random.uniform(jax.random.fold_in(own, dim), (blocks,), jnp.float32, smallest / len(shards), top_value / len(shards)))
        factor_of = factor_of * jnp.repeat(steps, shape[dim] // blocks).reshape([-1 if axis == dim else 1 for axis in range(len(shape))])
    return factor_of


def bell_draw(own_key, dims, scale, limit, cuts=(), dtype=jnp.bfloat16):
    drawn = scale * jax.random.normal(own_key, dims, jnp.float32)
    if cuts:
        drawn = drawn * block_levels(own_key, dims, cuts, -0.22, 0.18)
    return jnp.clip(drawn, -limit, limit).astype(dtype)


def setup_inputs(seed: int = 0) -> dict:
    key_of = jax.random.split(jax.random.key(seed), 8)
    query = draw_query(jax.random.fold_in(key_of[7], 71), 0)
    keys = draw_keys(jax.random.fold_in(key_of[7], 71), 0)
    values = bell_draw(key_of[2], (SEQS, MAX_LEN, KV_HEADS, HEAD_DIM), 1.0, 6.0, ((0, 4), (1, 8)))
    output = bell_draw(key_of[3], (SEQS, MAX_LEN, HEADS, HEAD_DIM), 1.0, 6.0, ((0, 4), (1, 8)))
    out_grad = bell_draw(key_of[4], (SEQS, MAX_LEN, HEADS, HEAD_DIM), 1.0, 6.0, ((0, 4), (1, 8)))
    lengths = draw_lengths(jax.random.fold_in(key_of[7], 71), 0)
    margins = jnp.clip(jax.random.uniform(key_of[6], (PAIRS,), jnp.float32, -3.0, 3.0) * block_levels(key_of[6], (PAIRS,), ((0, 4),), -0.4, 0.0), -3.0, 3.0)
    return dict(query=query, keys=keys, values=values, output=output, out_grad=out_grad, lengths=lengths, margins=margins)


def sequence_grads(query, scaled, keys, values, delta):
    full_len, heads, head_dim = query.shape
    slots = keys.shape[1]
    repeat = heads // slots
    block = min(512, full_len)
    scale = 1.0 / math.sqrt(head_dim)
    q_four = query.reshape(full_len, slots, repeat, head_dim).astype(jnp.float32)
    g_four = scaled.reshape(full_len, slots, repeat, head_dim).astype(jnp.float32)
    d_three = delta.reshape(full_len, slots, repeat)
    keys_wide = keys.astype(jnp.float32)
    values_wide = values.astype(jnp.float32)
    key_pos = jnp.arange(full_len)
    key_acc = jnp.zeros((full_len, slots, head_dim), jnp.float32)
    value_acc = jnp.zeros((full_len, slots, head_dim), jnp.float32)
    pieces = []
    for index in range(full_len // block):
        start = index * block
        q_block = q_four[start:start + block]
        g_block = g_four[start:start + block]
        d_block = jnp.transpose(d_three[start:start + block], (1, 2, 0))[..., None]
        scores = jnp.einsum('isrd,jsd->srij', q_block, keys_wide) * scale
        query_pos = start + jnp.arange(block)
        causal = key_pos[None, :] <= query_pos[:, None]
        scores = jnp.where(causal, scores, -jnp.inf)
        top = lax.optimization_barrier(jnp.max(scores, axis=-1, keepdims=True))
        lse = top + jnp.log(lax.optimization_barrier(jnp.sum(jnp.exp(scores - top), axis=-1, keepdims=True)))
        prob = jnp.exp(scores - lse)
        prob_low = lax.optimization_barrier(prob.astype(jnp.bfloat16)).astype(jnp.float32)
        value_acc = value_acc + jnp.einsum('srij,isrd->jsd', prob_low, g_block)
        dprob = jnp.einsum('isrd,jsd->srij', g_block, values_wide)
        dscore = prob * (dprob - d_block)
        dscore_low = lax.optimization_barrier(dscore.astype(jnp.bfloat16)).astype(jnp.float32)
        query_part = jnp.einsum('srij,jsd->isrd', dscore_low, keys_wide) * scale
        pieces.append(query_part.reshape(block, heads, head_dim).astype(jnp.bfloat16))
        key_acc = key_acc + jnp.einsum('srij,isrd->jsd', dscore_low, q_block)
    query_grad = jnp.concatenate(pieces, axis=0)
    return (query_grad, (key_acc * scale).astype(jnp.bfloat16), value_acc.astype(jnp.bfloat16))

def reference(query, keys, values, output, out_grad, lengths, margins):
    seqs = query.shape[0]
    total = jnp.sum(lengths)
    mean_len = total.astype(jnp.float32) / seqs
    weight = jax.nn.sigmoid(-margins)
    signs = jnp.tile(jnp.array([-1.0, 1.0], jnp.float32), margins.shape[0])
    coef = jnp.repeat(weight, 2) * signs * 4.0 * mean_len / lengths.astype(jnp.float32)
    live = (jnp.arange(MAX_LEN).astype(jnp.int32)[None, :] < lengths[:, None]).astype(jnp.float32)
    factor = coef[:, None] * live
    scaled = (out_grad.astype(jnp.float32) * factor[:, :, None, None]).astype(jnp.bfloat16)
    delta = lax.optimization_barrier(jnp.sum(scaled.astype(jnp.float32) * output.astype(jnp.float32), axis=3))
    query_grad, key_grad, value_grad = lax.map(lambda items: sequence_grads(*items), (query, scaled, keys, values, delta))
    return (query_grad, key_grad, value_grad)
```

```python
import functools
import math

import jax
import jax.numpy as jnp
from jax import lax
from jax.experimental import pallas as pl
from jax.experimental.pallas import tpu as pltpu
from jax.sharding import PartitionSpec as P

CHUNK_TOKENS = 64
KEY_BLOCK = 1024
LOW = -1e30
MESH = pl.DeviceIdType.MESH
NT = (((1,), (1,)), ((), ()))
TN = (((0,), (0,)), ((), ()))


def dot(a, b, dims=(((1,), (0,)), ((), ()))):
    return lax.dot_general(a, b, dims, preferred_element_type=jnp.float32)


def fused_kernel(
    lengths,
    coef,
    query,
    grad,
    output,
    kv,
    query_grad,
    kv_grad,
    blocks,
    parts,
    z_in,
    x_in,
    q_buf,
    g_buf,
    o_buf,
    dq_buf,
    s_ref,
    e_ref,
    ds_ref,
    key_acc,
    value_acc,
    wide,
    own_sem,
    load_sem,
    store_sem,
    up_send,
    across_send,
    block_recv,
    down_send,
    side_send,
    down_recv,
    side_recv,
    out_sem,
    *,
    scale,
    chunk_tokens,
    key_block,
):
    items, slots, _, toks, dim = blocks.shape
    group = q_buf.shape[2]
    kv_heads = items // query.shape[0]
    levels = slots // 2
    rows = chunk_tokens * group
    count = slots * toks
    log2e = scale * math.log2(math.e)

    me = lax.axis_index("seq")
    level = me // 2
    side = me % 2
    has_up = level < levels - 1
    has_down = level >= 1
    above = jnp.minimum(me + 2, slots - 1)
    below = jnp.maximum(me - 2, 0)
    beside = me + 1 - 2 * side

    def remote(src, dst, send, recv, place):
        return pltpu.make_async_remote_copy(
            src_ref=src,
            dst_ref=dst,
            send_sem=send,
            recv_sem=recv,
            device_id={"seq": place},
            device_id_type=MESH,
        )

    def up(i, r):
        src = kv.at[i] if r == 0 else blocks.at[i, r]
        return remote(src, blocks.at[i, r + 2], up_send.at[i, r], block_recv.at[i, r + 2], above)

    def across(i, r):
        to = r + 1 - 2 * side if r else 1
        src = kv.at[i] if r == 0 else blocks.at[i, r]
        return remote(
            src, blocks.at[i, to], across_send.at[i, r // 2], block_recv.at[i, to], beside
        )

    def arrived(i, r):
        remote(
            blocks.at[i, r], blocks.at[i, r], up_send.at[i, r], block_recv.at[i, r], beside
        ).wait_recv()

    def down(i, r):
        return remote(
            parts.at[i, r], z_in.at[i, r - 2], down_send.at[i, r], down_recv.at[i, r - 2], below
        )

    def sideways(i, r):
        to = 1 - side if r == 1 else 1
        return remote(
            parts.at[i, r], x_in.at[i, to], side_send.at[i, r // 2], side_recv.at[i, to], beside
        )

    def own(i):
        return pltpu.make_async_copy(kv.at[i], blocks.at[i, 0], own_sem.at[i])

    def loads(i):
        slot = i % 2
        seq = i // kv_heads
        heads = pl.ds(pl.multiple_of(i % kv_heads * group, group), group)
        return [
            pltpu.make_async_copy(
                array.at[seq, :, heads], buf.at[slot], load_sem.at[slot, which]
            )
            for which, (array, buf) in enumerate(
                ((query, q_buf), (grad, g_buf), (output, o_buf))
            )
        ]

    def store(i):
        slot = i % 2
        seq = i // kv_heads
        heads = pl.ds(pl.multiple_of(i % kv_heads * group, group), group)
        return pltpu.make_async_copy(
            dq_buf.at[slot], query_grad.at[seq, :, heads], store_sem.at[slot]
        )

    def result(i):
        return pltpu.make_async_copy(parts.at[i, 0], kv_grad.at[i], out_sem.at[i])

    barrier = pltpu.get_barrier_semaphore()
    pl.semaphore_signal(barrier, inc=1, device_id={"seq": beside}, device_id_type=MESH)

    @pl.when(has_up)
    def _():
        pl.semaphore_signal(barrier, inc=1, device_id={"seq": above}, device_id_type=MESH)

    @pl.when(has_down)
    def _():
        pl.semaphore_signal(barrier, inc=1, device_id={"seq": below}, device_id_type=MESH)

    def start_own(i, _):
        own(i).start()
        return 0

    lax.fori_loop(0, items, start_own, 0)
    for copy in loads(0):
        copy.start()

    peers = 1 + has_up.astype(jnp.int32) + has_down.astype(jnp.int32)
    pl.semaphore_wait(barrier, peers)

    def start_sends(i, _):
        @pl.when(side == 0)
        def _():
            across(i, 0).start()

        @pl.when(has_up)
        def _():
            up(i, 0).start()

        return 0

    lax.fori_loop(0, items, start_sends, 0)

    lane = lax.broadcasted_iota(jnp.int32, (count, dim), 1)
    wide[:, dim:] = jnp.where(lane < 3, 1.0, 0.0).astype(jnp.bfloat16)
    for r in range(1, slots):

        @pl.when(r > me)
        def _():
            def clear(i, _):
                blocks[i, r] = jnp.zeros(blocks.shape[2:], blocks.dtype)
                return 0

            lax.fori_loop(0, items, clear, 0)

    def forward(i):
        for r in [2, 1] + list(range(3, slots)):

            @pl.when(me >= r)
            def _():
                arrived(i, r)
                if r == 2:
                    across(i, r).start()
                if r + 2 < slots:

                    @pl.when(has_up & (side == 0) if r == 1 else has_up)
                    def _():
                        up(i, r).start()

    def keys_of(i, start):
        return jnp.concatenate(
            [blocks[i, r, 0] for r in range(start // toks, (start + key_block) // toks)], axis=0
        )

    def compute(i):
        slot = i % 2
        seq = i // kv_heads
        length = lengths[seq]
        factor_live = coef[seq]
        base = me * toks
        for r in range(slots):
            wide[r * toks : (r + 1) * toks, :dim] = blocks[i, r, 1]
        key_acc[...] = jnp.zeros((count, dim), jnp.float32)
        value_acc[...] = jnp.zeros((count, dim), jnp.float32)

        def chunk(ch, _):
            tok0 = pl.multiple_of(ch * chunk_tokens, chunk_tokens)
            here = pl.ds(tok0, chunk_tokens)
            q_wide = q_buf[slot, here].astype(jnp.float32).reshape(rows, dim)
            q = q_wide.astype(jnp.bfloat16)
            position = (
                base + tok0 + lax.broadcasted_iota(jnp.int32, (chunk_tokens, group, dim), 0)
            )
            factor = jnp.where(position < length, factor_live, 0.0)
            g = (
                (g_buf[slot, here].astype(jnp.float32) * factor)
                .reshape(rows, dim)
                .astype(jnp.bfloat16)
            )
            g_f32 = g.astype(jnp.float32)
            o = o_buf[slot, here].astype(jnp.float32).reshape(rows, dim)
            delta = jnp.sum(g_f32 * o, axis=-1, keepdims=True)
            high = delta.astype(jnp.bfloat16).astype(jnp.float32)
            middle = (delta - high).astype(jnp.bfloat16).astype(jnp.float32)
            low = delta - high - middle
            row_lane = lax.broadcasted_iota(jnp.int32, (rows, dim), 1)
            extra = jnp.where(
                row_lane == 0,
                -high,
                jnp.where(row_lane == 1, -middle, jnp.where(row_lane == 2, -low, 0.0)),
            ).astype(jnp.bfloat16)
            g_wide = jnp.concatenate([g, extra], axis=1)

            top = jnp.full((8, rows), LOW, jnp.float32)
            for start in range(0, count, key_block):
                scores = dot(keys_of(i, start), q, NT)
                for r in range(start // toks, (start + key_block) // toks):
                    part = scores[r * toks - start : (r + 1) * toks - start]
                    if r == 0:
                        key_row = lax.broadcasted_iota(jnp.int32, (toks, rows), 0)
                        row_pos = (
                            tok0 + lax.broadcasted_iota(jnp.int32, (toks, rows), 1) // group
                        )
                        part = jnp.where(key_row <= row_pos, part, LOW)
                    s_ref[r * toks : (r + 1) * toks] = part
                    best = jnp.max(part.reshape(-1, 8, rows), axis=0)
                    if r:
                        best = jnp.where(r <= me, best, LOW)
                    top = jnp.maximum(top, best)
            top = jnp.max(top, axis=0, keepdims=True) * log2e

            total = jnp.zeros((8, rows), jnp.float32)
            for start in range(0, count, key_block):
                span = slice(start, start + key_block)
                dprob = dot(wide[span], g_wide, NT)
                for r in range(start // toks, (start + key_block) // toks):
                    here_keys = slice(r * toks, (r + 1) * toks)
                    shift = jnp.where(r <= me, top, -LOW) if r else top
                    e = jnp.exp2(s_ref[here_keys] * log2e - shift)
                    total = total + jnp.sum(e.reshape(-1, 8, rows), axis=0)
                    e_ref[here_keys] = e.astype(jnp.bfloat16)
                    ds_ref[here_keys] = (
                        e * dprob[r * toks - start : (r + 1) * toks - start]
                    ).astype(jnp.bfloat16)
            keys_all = jnp.concatenate([blocks[i, r, 0] for r in range(slots)], axis=0)
            acc = dot(keys_all, ds_ref[...], TN)
            inverse = 1.0 / jnp.sum(total, axis=0, keepdims=True)
            columns = jnp.broadcast_to(inverse, (dim, rows)).T
            dq = (acc * (inverse * scale)).T
            dq_buf[slot, here] = dq.reshape(chunk_tokens, group, dim).astype(dq_buf.dtype)
            q_low = (q_wide * columns).astype(jnp.bfloat16)
            g_low = (g_f32 * columns).astype(jnp.bfloat16)
            value_acc[...] += dot(e_ref[...], g_low)
            key_acc[...] += dot(ds_ref[...], q_low)
            return 0

        lax.fori_loop(0, toks // chunk_tokens, chunk, 0)
        for r in range(slots):
            span = slice(r * toks, (r + 1) * toks)
            parts[i, r, 0] = (key_acc[span] * scale).astype(parts.dtype)
            parts[i, r, 1] = value_acc[span].astype(parts.dtype)

    def add(i, r, extra):
        parts[i, r] = (parts[i, r].astype(jnp.float32) + extra.astype(jnp.float32)).astype(
            parts.dtype
        )

    def add_down(i, r):
        remote(
            parts.at[i, r], z_in.at[i, r], down_send.at[i, r], down_recv.at[i, r], beside
        ).wait_recv()
        add(i, r, z_in[i, r])

    def add_side(i, r, to):
        remote(
            parts.at[i, r], x_in.at[i, to], side_send.at[i, to], side_recv.at[i, to], beside
        ).wait_recv()
        add(i, r, x_in[i, to])

    def reduce_first(i):
        for r in [3, 1] + list(range(4, slots)):

            @pl.when(me >= r)
            def _():
                if r + 2 < slots:

                    @pl.when(has_up & (side == 0) if r == 1 else has_up)
                    def _():
                        add_down(i, r)

                if r == 1:
                    sideways(i, r).start()
                elif r == 3:

                    @pl.when(side == 1)
                    def _():
                        sideways(i, r).start()

                    @pl.when(side == 0)
                    def _():
                        down(i, r).start()

                else:
                    down(i, r).start()

    def reduce_second(i):
        @pl.when(has_down)
        def _():
            @pl.when(has_up)
            def _():
                add_down(i, 2)

            add_side(i, 2, 1)
            down(i, 2).start()

        @pl.when(has_up)
        def _():
            add_down(i, 0)

        @pl.when(side == 0)
        def _():
            add_side(i, 0, 0)

        result(i).start()

    ahead = levels - 1 - level
    lag = 2 * ahead

    def step(u, _):
        t = u - (levels - 1)
        f = u - level

        @pl.when((f >= 0) & (f < items))
        def _():
            forward(f)

        @pl.when((t >= 0) & (t < items))
        def _():
            own(t).wait()
            for copy in loads(t):
                copy.wait()

            @pl.when(t + 1 < items)
            def _():
                for copy in loads(t + 1):
                    copy.start()

            @pl.when(t >= 2)
            def _():
                store(t - 2).wait()

            compute(t)
            store(t).start()

        @pl.when((t - lag >= 0) & (t - lag < items))
        def _():
            reduce_first(t - lag)

        @pl.when((t - lag - 1 >= 0) & (t - lag - 1 < items))
        def _():
            reduce_second(t - lag - 1)

        return 0

    lax.fori_loop(0, items + 3 * levels - 2, step, 0)

    for i in range(max(items - 2, 0), items):
        store(i).wait()

    def finish(i, _):
        result(i).wait()

        @pl.when(side == 0)
        def _():
            across(i, 0).wait_send()

        @pl.when(has_up)
        def _():
            up(i, 0).wait_send()

        for r in range(1, slots):

            @pl.when(me >= r)
            def _():
                if r == 2:
                    across(i, r).wait_send()
                if r + 2 < slots:

                    @pl.when(has_up & (side == 0) if r == 1 else has_up)
                    def _():
                        up(i, r).wait_send()

                if r == 1:
                    sideways(i, r).wait_send()
                elif r == 3:

                    @pl.when(side == 1)
                    def _():
                        sideways(i, r).wait_send()

                    @pl.when(side == 0)
                    def _():
                        down(i, r).wait_send()

                else:
                    down(i, r).wait_send()

        return 0

    lax.fori_loop(0, items, finish, 0)


def fused(lengths, coef, query, grad, output, kv, slots):
    items, _, toks, dim = kv.shape
    seqs, _, heads, _ = query.shape
    group = heads * seqs // items
    count = slots * toks
    chunk_tokens = min(CHUNK_TOKENS, toks)
    rows = chunk_tokens * group
    key_block = max(toks, min(KEY_BLOCK, count))
    bf16 = jnp.bfloat16
    block = (2, toks, dim)
    dma = pltpu.SemaphoreType.DMA
    anywhere = pl.BlockSpec(memory_space=pl.ANY)
    smem = pl.BlockSpec(memory_space=pltpu.SMEM)
    return pl.pallas_call(
        functools.partial(
            fused_kernel,
            scale=1.0 / math.sqrt(dim),
            chunk_tokens=chunk_tokens,
            key_block=key_block,
        ),
        out_shape=(
            jax.ShapeDtypeStruct(query.shape, bf16),
            jax.ShapeDtypeStruct(kv.shape, bf16),
        ),
        in_specs=[smem] * 2 + [anywhere] * 4,
        out_specs=(anywhere,) * 2,
        scratch_shapes=[
            pltpu.VMEM((items, slots) + block, bf16),
            pltpu.VMEM((items, slots) + block, bf16),
            pltpu.VMEM((items, slots - 2) + block, bf16),
            pltpu.VMEM((items, 2) + block, bf16),
            pltpu.VMEM((2, toks, group, dim), bf16),
            pltpu.VMEM((2, toks, group, dim), bf16),
            pltpu.VMEM((2, toks, group, dim), bf16),
            pltpu.VMEM((2, toks, group, dim), bf16),
            pltpu.VMEM((count, rows), jnp.float32),
            pltpu.VMEM((count, rows), bf16),
            pltpu.VMEM((count, rows), bf16),
            pltpu.VMEM((count, dim), jnp.float32),
            pltpu.VMEM((count, dim), jnp.float32),
            pltpu.VMEM((count, 2 * dim), bf16),
            dma((items,)),
            dma((2, 3)),
            dma((2,)),
            dma((items, slots)),
            dma((items, 2)),
            dma((items, slots)),
            dma((items, slots)),
            dma((items, 2)),
            dma((items, slots)),
            dma((items, 2)),
            dma((items,)),
        ],
        compiler_params=pltpu.CompilerParams(
            collective_id=0, has_side_effects=True, vmem_limit_bytes=62 * 1024 * 1024
        ),
    )(lengths, coef, query, grad, output, kv)


def body(query, keys, values, output, out_grad, lengths, margins):
    slots = lax.axis_size("seq")
    seqs, toks, heads, dim = query.shape
    kv_heads = keys.shape[2]
    kv = jnp.stack([keys, values], axis=1).transpose(0, 3, 1, 2, 4)
    kv = kv.reshape(seqs * kv_heads, 2, toks, dim)
    total = lax.psum(jnp.sum(lengths), "dp")
    mean_len = total.astype(jnp.float32) / (seqs * lax.axis_size("dp"))
    weight = jax.nn.sigmoid(-margins)
    signs = jnp.tile(jnp.array([-1.0, 1.0], jnp.float32), margins.shape[0])
    coef = jnp.repeat(weight, 2) * signs * 4.0 * mean_len / lengths.astype(jnp.float32)
    query_grad, grads = fused(lengths, coef, query, out_grad, output, kv, slots)
    grads = grads.reshape(seqs, kv_heads, 2, toks, dim)
    key_grad = grads[:, :, 0].transpose(0, 2, 1, 3)
    value_grad = grads[:, :, 1].transpose(0, 2, 1, 3)
    return (query_grad, key_grad, value_grad)


def solution(mesh):
    tokens = P("dp", "seq", None, None)
    return jax.shard_map(
        body,
        mesh=mesh,
        in_specs=(tokens,) * 5 + (P("dp"), P("dp")),
        out_specs=(tokens,) * 3,
        check_vma=False,
    )
```

```python
import functools
import math

import jax
import jax.numpy as jnp
from jax import lax
from jax.experimental import pallas as pl
from jax.experimental.pallas import tpu as pltpu
from jax.sharding import PartitionSpec as P

CHUNK_TOKENS = 64
KEY_BLOCK = 1024
LOW = -1e30
MESH = pl.DeviceIdType.MESH
NT = (((1,), (1,)), ((), ()))
TN = (((0,), (0,)), ((), ()))


def dot(a, b, dims=(((1,), (0,)), ((), ()))):
    return lax.dot_general(a, b, dims, preferred_element_type=jnp.float32)


def fused_kernel(
    lengths,
    coef,
    query,
    grad,
    output,
    kv,
    query_grad,
    kv_grad,
    blocks,
    parts,
    z_in,
    x_in,
    q_buf,
    g_buf,
    o_buf,
    dq_buf,
    s_ref,
    e_ref,
    ds_ref,
    key_acc,
    value_acc,
    wide,
    own_sem,
    load_sem,
    store_sem,
    up_send,
    across_send,
    block_recv,
    down_send,
    side_send,
    down_recv,
    side_recv,
    out_sem,
    *,
    scale,
    chunk_tokens,
    key_block,
):
    items, slots, _, toks, dim = blocks.shape
    group = q_buf.shape[2]
    kv_heads = items // query.shape[0]
    levels = slots // 2
    rows = chunk_tokens * group
    count = slots * toks
    log2e = scale * math.log2(math.e)

    me = lax.axis_index("seq")
    level = me // 2
    side = me % 2
    has_up = level < levels - 1
    has_down = level >= 1
    above = jnp.minimum(me + 2, slots - 1)
    below = jnp.maximum(me - 2, 0)
    beside = me + 1 - 2 * side

    def remote(src, dst, send, recv, place):
        return pltpu.make_async_remote_copy(
            src_ref=src,
            dst_ref=dst,
            send_sem=send,
            recv_sem=recv,
            device_id={"seq": place},
            device_id_type=MESH,
        )

    def up(i, r):
        src = kv.at[i] if r == 0 else blocks.at[i, r]
        return remote(src, blocks.at[i, r + 2], up_send.at[i, r], block_recv.at[i, r + 2], above)

    def across(i, r):
        to = r + 1 - 2 * side if r else 1
        src = kv.at[i] if r == 0 else blocks.at[i, r]
        return remote(
            src, blocks.at[i, to], across_send.at[i, r // 2], block_recv.at[i, to], beside
        )

    def arrived(i, r):
        remote(
            blocks.at[i, r], blocks.at[i, r], up_send.at[i, r], block_recv.at[i, r], beside
        ).wait_recv()

    def down(i, r):
        return remote(
            parts.at[i, r], z_in.at[i, r - 2], down_send.at[i, r], down_recv.at[i, r - 2], below
        )

    def sideways(i, r):
        to = 1 - side if r == 1 else 1
        return remote(
            parts.at[i, r], x_in.at[i, to], side_send.at[i, r // 2], side_recv.at[i, to], beside
        )

    def own(i):
        return pltpu.make_async_copy(kv.at[i], blocks.at[i, 0], own_sem.at[i])

    def loads(i):
        slot = i % 2
        seq = i // kv_heads
        heads = pl.ds(pl.multiple_of(i % kv_heads * group, group), group)
        return [
            pltpu.make_async_copy(
                array.at[seq, :, heads], buf.at[slot], load_sem.at[slot, which]
            )
            for which, (array, buf) in enumerate(
                ((query, q_buf), (grad, g_buf), (output, o_buf))
            )
        ]

    def store(i):
        slot = i % 2
        seq = i // kv_heads
        heads = pl.ds(pl.multiple_of(i % kv_heads * group, group), group)
        return pltpu.make_async_copy(
            dq_buf.at[slot], query_grad.at[seq, :, heads], store_sem.at[slot]
        )

    def result(i):
        return pltpu.make_async_copy(parts.at[i, 0], kv_grad.at[i], out_sem.at[i])

    barrier = pltpu.get_barrier_semaphore()
    pl.semaphore_signal(barrier, inc=1, device_id={"seq": beside}, device_id_type=MESH)

    @pl.when(has_up)
    def _():
        pl.semaphore_signal(barrier, inc=1, device_id={"seq": above}, device_id_type=MESH)

    @pl.when(has_down)
    def _():
        pl.semaphore_signal(barrier, inc=1, device_id={"seq": below}, device_id_type=MESH)

    def start_own(i, _):
        own(i).start()
        return 0

    lax.fori_loop(0, items, start_own, 0)
    for copy in loads(0):
        copy.start()

    peers = 1 + has_up.astype(jnp.int32) + has_down.astype(jnp.int32)
    pl.semaphore_wait(barrier, peers)

    def start_sends(i):
        @pl.when(side == 0)
        def _():
            across(i, 0).start()

        @pl.when(has_up)
        def _():
            up(i, 0).start()

    for i in range(min(2, items)):
        start_sends(i)

    lane = lax.broadcasted_iota(jnp.int32, (count, dim), 1)
    wide[:, dim:] = jnp.where(lane < 3, 1.0, 0.0).astype(jnp.bfloat16)
    for r in range(1, slots):

        @pl.when(r > me)
        def _():
            def clear(i, _):
                blocks[i, r] = jnp.zeros(blocks.shape[2:], blocks.dtype)
                return 0

            lax.fori_loop(0, items, clear, 0)

    def forward_first(i):
        arrived(i, 2)
        across(i, 2).start()

        @pl.when(has_up)
        def _():
            up(i, 2).start()

    def forward_rest(i):
        for r in [1] + list(range(3, slots)):

            @pl.when(me >= r)
            def _():
                arrived(i, r)
                if r + 2 < slots:

                    @pl.when(has_up & (side == 0) if r == 1 else has_up)
                    def _():
                        up(i, r).start()

    def keys_of(i, start):
        return jnp.concatenate(
            [blocks[i, r, 0] for r in range(start // toks, (start + key_block) // toks)], axis=0
        )

    def compute(i):
        slot = i % 2
        seq = i // kv_heads
        length = lengths[seq]
        factor_live = coef[seq]
        base = me * toks
        for r in range(slots):
            wide[r * toks : (r + 1) * toks, :dim] = blocks[i, r, 1]
        key_acc[...] = jnp.zeros((count, dim), jnp.float32)
        value_acc[...] = jnp.zeros((count, dim), jnp.float32)

        def chunk(ch, _):
            tok0 = pl.multiple_of(ch * chunk_tokens, chunk_tokens)
            here = pl.ds(tok0, chunk_tokens)
            q_wide = q_buf[slot, here].astype(jnp.float32).reshape(rows, dim)
            q = q_wide.astype(jnp.bfloat16)
            position = (
                base + tok0 + lax.broadcasted_iota(jnp.int32, (chunk_tokens, group, dim), 0)
            )
            factor = jnp.where(position < length, factor_live, 0.0)
            g = (
                (g_buf[slot, here].astype(jnp.float32) * factor)
                .reshape(rows, dim)
                .astype(jnp.bfloat16)
            )
            g_f32 = g.astype(jnp.float32)
            o = o_buf[slot, here].astype(jnp.float32).reshape(rows, dim)
            delta = jnp.sum(g_f32 * o, axis=-1, keepdims=True)
            high = delta.astype(jnp.bfloat16).astype(jnp.float32)
            middle = (delta - high).astype(jnp.bfloat16).astype(jnp.float32)
            low = delta - high - middle
            row_lane = lax.broadcasted_iota(jnp.int32, (rows, dim), 1)
            extra = jnp.where(
                row_lane == 0,
                -high,
                jnp.where(row_lane == 1, -middle, jnp.where(row_lane == 2, -low, 0.0)),
            ).astype(jnp.bfloat16)
            g_wide = jnp.concatenate([g, extra], axis=1)

            top = jnp.full((8, rows), LOW, jnp.float32)
            for start in range(0, count, key_block):
                scores = dot(keys_of(i, start), q, NT)
                for r in range(start // toks, (start + key_block) // toks):
                    part = scores[r * toks - start : (r + 1) * toks - start]
                    if r == 0:
                        key_row = lax.broadcasted_iota(jnp.int32, (toks, rows), 0)
                        row_pos = (
                            tok0 + lax.broadcasted_iota(jnp.int32, (toks, rows), 1) // group
                        )
                        part = jnp.where(key_row <= row_pos, part, LOW)
                    s_ref[r * toks : (r + 1) * toks] = part
                    best = jnp.max(part.reshape(-1, 8, rows), axis=0)
                    if r:
                        best = jnp.where(r <= me, best, LOW)
                    top = jnp.maximum(top, best)
            top = jnp.max(top, axis=0, keepdims=True) * log2e

            total = jnp.zeros((8, rows), jnp.float32)
            for start in range(0, count, key_block):
                span = slice(start, start + key_block)
                dprob = dot(wide[span], g_wide, NT)
                for r in range(start // toks, (start + key_block) // toks):
                    here_keys = slice(r * toks, (r + 1) * toks)
                    shift = jnp.where(r <= me, top, -LOW) if r else top
                    e = jnp.exp2(s_ref[here_keys] * log2e - shift)
                    total = total + jnp.sum(e.reshape(-1, 8, rows), axis=0)
                    e_ref[here_keys] = e.astype(jnp.bfloat16)
                    ds_ref[here_keys] = (
                        e * dprob[r * toks - start : (r + 1) * toks - start]
                    ).astype(jnp.bfloat16)
            keys_all = jnp.concatenate([blocks[i, r, 0] for r in range(slots)], axis=0)
            acc = dot(keys_all, ds_ref[...], TN)
            inverse = 1.0 / jnp.sum(total, axis=0, keepdims=True)
            columns = jnp.broadcast_to(inverse, (dim, rows)).T
            dq = (acc * (inverse * scale)).T
            dq_buf[slot, here] = dq.reshape(chunk_tokens, group, dim).astype(dq_buf.dtype)
            q_low = (q_wide * columns).astype(jnp.bfloat16)
            g_low = (g_f32 * columns).astype(jnp.bfloat16)
            value_acc[...] += dot(e_ref[...], g_low)
            key_acc[...] += dot(ds_ref[...], q_low)
            return 0

        lax.fori_loop(0, toks // chunk_tokens, chunk, 0)
        for r in range(slots):
            span = slice(r * toks, (r + 1) * toks)
            parts[i, r, 0] = (key_acc[span] * scale).astype(parts.dtype)
            parts[i, r, 1] = value_acc[span].astype(parts.dtype)

    def add(i, r, extra):
        parts[i, r] = (parts[i, r].astype(jnp.float32) + extra.astype(jnp.float32)).astype(
            parts.dtype
        )

    def add_down(i, r):
        remote(
            parts.at[i, r], z_in.at[i, r], down_send.at[i, r], down_recv.at[i, r], beside
        ).wait_recv()
        add(i, r, z_in[i, r])

    def add_side(i, r, to):
        remote(
            parts.at[i, r], x_in.at[i, to], side_send.at[i, to], side_recv.at[i, to], beside
        ).wait_recv()
        add(i, r, x_in[i, to])

    def reduce_first(i):
        for r in [3, 1] + list(range(slots - 1, 3, -1)):

            @pl.when(me >= r)
            def _():
                if r + 2 < slots:

                    @pl.when(has_up & (side == 0) if r == 1 else has_up)
                    def _():
                        add_down(i, r)

                if r == 1:
                    sideways(i, r).start()
                elif r == 3:

                    @pl.when(side == 1)
                    def _():
                        sideways(i, r).start()

                    @pl.when(side == 0)
                    def _():
                        down(i, r).start()

                else:
                    down(i, r).start()

    def reduce_second(i):
        @pl.when(has_down)
        def _():
            @pl.when(has_up)
            def _():
                add_down(i, 2)

            add_side(i, 2, 1)
            down(i, 2).start()

        @pl.when(has_up)
        def _():
            add_down(i, 0)

        @pl.when(side == 0)
        def _():
            add_side(i, 0, 0)

        result(i).start()

    ahead = levels - 1 - level
    lag = 2 * ahead

    def step(u, _):
        t = u - (levels - 1)
        f = u - level

        @pl.when((f >= 0) & (f < items))
        def _():
            forward_rest(f)

        @pl.when((f >= -1) & (f < items - 1) & has_down)
        def _():
            forward_first(f + 1)

        @pl.when((f >= 0) & (f < items - 2))
        def _():
            start_sends(f + 2)

        @pl.when((t >= 0) & (t < items))
        def _():
            own(t).wait()
            for copy in loads(t):
                copy.wait()

            @pl.when(t + 1 < items)
            def _():
                for copy in loads(t + 1):
                    copy.start()

            @pl.when(t >= 2)
            def _():
                store(t - 2).wait()

            compute(t)
            store(t).start()

        @pl.when((t - lag >= 0) & (t - lag < items))
        def _():
            reduce_first(t - lag)

        @pl.when((t - lag - 1 >= 0) & (t - lag - 1 < items))
        def _():
            reduce_second(t - lag - 1)

        return 0

    lax.fori_loop(0, items + 3 * levels - 2, step, 0)

    for i in range(max(items - 2, 0), items):
        store(i).wait()

    def finish(i, _):
        result(i).wait()

        @pl.when(side == 0)
        def _():
            across(i, 0).wait_send()

        @pl.when(has_up)
        def _():
            up(i, 0).wait_send()

        for r in range(1, slots):

            @pl.when(me >= r)
            def _():
                if r == 2:
                    across(i, r).wait_send()
                if r + 2 < slots:

                    @pl.when(has_up & (side == 0) if r == 1 else has_up)
                    def _():
                        up(i, r).wait_send()

                if r == 1:
                    sideways(i, r).wait_send()
                elif r == 3:

                    @pl.when(side == 1)
                    def _():
                        sideways(i, r).wait_send()

                    @pl.when(side == 0)
                    def _():
                        down(i, r).wait_send()

                else:
                    down(i, r).wait_send()

        return 0

    lax.fori_loop(0, items, finish, 0)


def fused(lengths, coef, query, grad, output, kv, slots):
    items, _, toks, dim = kv.shape
    seqs, _, heads, _ = query.shape
    group = heads * seqs // items
    count = slots * toks
    chunk_tokens = min(CHUNK_TOKENS, toks)
    rows = chunk_tokens * group
    key_block = max(toks, min(KEY_BLOCK, count))
    bf16 = jnp.bfloat16
    block = (2, toks, dim)
    dma = pltpu.SemaphoreType.DMA
    anywhere = pl.BlockSpec(memory_space=pl.ANY)
    smem = pl.BlockSpec(memory_space=pltpu.SMEM)
    return pl.pallas_call(
        functools.partial(
            fused_kernel,
            scale=1.0 / math.sqrt(dim),
            chunk_tokens=chunk_tokens,
            key_block=key_block,
        ),
        out_shape=(
            jax.ShapeDtypeStruct(query.shape, bf16),
            jax.ShapeDtypeStruct(kv.shape, bf16),
        ),
        in_specs=[smem] * 2 + [anywhere] * 4,
        out_specs=(anywhere,) * 2,
        scratch_shapes=[
            pltpu.VMEM((items, slots) + block, bf16),
            pltpu.VMEM((items, slots) + block, bf16),
            pltpu.VMEM((items, slots - 2) + block, bf16),
            pltpu.VMEM((items, 2) + block, bf16),
            pltpu.VMEM((2, toks, group, dim), bf16),
            pltpu.VMEM((2, toks, group, dim), bf16),
            pltpu.VMEM((2, toks, group, dim), bf16),
            pltpu.VMEM((2, toks, group, dim), bf16),
            pltpu.VMEM((count, rows), jnp.float32),
            pltpu.VMEM((count, rows), bf16),
            pltpu.VMEM((count, rows), bf16),
            pltpu.VMEM((count, dim), jnp.float32),
            pltpu.VMEM((count, dim), jnp.float32),
            pltpu.VMEM((count, 2 * dim), bf16),
            dma((items,)),
            dma((2, 3)),
            dma((2,)),
            dma((items, slots)),
            dma((items, 2)),
            dma((items, slots)),
            dma((items, slots)),
            dma((items, 2)),
            dma((items, slots)),
            dma((items, 2)),
            dma((items,)),
        ],
        compiler_params=pltpu.CompilerParams(
            collective_id=0,
            has_side_effects=True,
            vmem_limit_bytes=62 * 1024 * 1024,
        ),
    )(lengths, coef, query, grad, output, kv)


def body(query, keys, values, output, out_grad, lengths, margins):
    slots = lax.axis_size("seq")
    seqs, toks, heads, dim = query.shape
    kv_heads = keys.shape[2]
    kv = jnp.stack([keys, values], axis=1).transpose(0, 3, 1, 2, 4)
    kv = kv.reshape(seqs * kv_heads, 2, toks, dim)
    total = lax.psum(jnp.sum(lengths), "dp")
    mean_len = total.astype(jnp.float32) / (seqs * lax.axis_size("dp"))
    weight = jax.nn.sigmoid(-margins)
    signs = jnp.tile(jnp.array([-1.0, 1.0], jnp.float32), margins.shape[0])
    coef = jnp.repeat(weight, 2) * signs * 4.0 * mean_len / lengths.astype(jnp.float32)
    query_grad, grads = fused(lengths, coef, query, out_grad, output, kv, slots)
    grads = grads.reshape(seqs, kv_heads, 2, toks, dim)
    key_grad = grads[:, :, 0].transpose(0, 2, 1, 3)
    value_grad = grads[:, :, 1].transpose(0, 2, 1, 3)
    return (query_grad, key_grad, value_grad)


def solution(mesh):
    tokens = P("dp", "seq", None, None)
    return jax.shard_map(
        body,
        mesh=mesh,
        in_specs=(tokens,) * 5 + (P("dp"), P("dp")),
        out_specs=(tokens,) * 3,
        check_vma=False,
    )
```

```python
import functools
import math

import jax
import jax.numpy as jnp
from jax import lax
from jax.experimental import pallas as pl
from jax.experimental.pallas import tpu as pltpu
from jax.sharding import PartitionSpec as P

CHUNK_TOKENS = 128
KEY_BLOCK = 1024
LOW = -1e30
MESH = pl.DeviceIdType.MESH
NT = (((1,), (1,)), ((), ()))
TN = (((0,), (0,)), ((), ()))


def dot(a, b, dims=(((1,), (0,)), ((), ()))):
    return lax.dot_general(a, b, dims, preferred_element_type=jnp.float32)


def fused_kernel(
    lengths,
    coef,
    tally,
    query,
    grad,
    output,
    kv,
    query_grad,
    kv_grad,
    blocks,
    parts,
    z_in,
    x_in,
    q_buf,
    g_buf,
    o_buf,
    dq_buf,
    s_ref,
    e_ref,
    ds_ref,
    key_acc,
    value_acc,
    wide,
    counts,
    mean,
    own_sem,
    load_sem,
    store_sem,
    up_send,
    across_send,
    block_recv,
    down_send,
    side_send,
    down_recv,
    side_recv,
    out_sem,
    count_sem,
    count_send,
    count_recv,
    *,
    scale,
    chunk_tokens,
    key_block,
):
    items, slots, _, toks, dim = blocks.shape
    group = q_buf.shape[2]
    kv_heads = items // query.shape[0]
    levels = slots // 2
    rows = chunk_tokens * group
    count = slots * toks
    log2e = scale * math.log2(math.e)

    groups = counts.shape[0]
    me = lax.axis_index("seq")
    level = me // 2
    side = me % 2
    has_up = level < levels - 1
    has_down = level >= 1
    above = jnp.minimum(me + 2, slots - 1)
    below = jnp.maximum(me - 2, 0)
    beside = me + 1 - 2 * side

    def remote(src, dst, send, recv, place):
        return pltpu.make_async_remote_copy(
            src_ref=src,
            dst_ref=dst,
            send_sem=send,
            recv_sem=recv,
            device_id={"seq": place},
            device_id_type=MESH,
        )

    def up(i, r):
        src = kv.at[i] if r == 0 else blocks.at[i, r]
        return remote(src, blocks.at[i, r + 2], up_send.at[i, r], block_recv.at[i, r + 2], above)

    def across(i, r):
        to = r + 1 - 2 * side if r else 1
        src = kv.at[i] if r == 0 else blocks.at[i, r]
        return remote(
            src, blocks.at[i, to], across_send.at[i, r // 2], block_recv.at[i, to], beside
        )

    def arrived(i, r):
        remote(
            blocks.at[i, r], blocks.at[i, r], up_send.at[i, r], block_recv.at[i, r], beside
        ).wait_recv()

    def down(i, r):
        return remote(
            parts.at[i, r], z_in.at[i, r - 2], down_send.at[i, r], down_recv.at[i, r - 2], below
        )

    def sideways(i, r):
        to = 1 - side if r == 1 else (2 - side if r == 3 else 2)
        return remote(
            parts.at[i, r], x_in.at[i, to], side_send.at[i, r // 2], side_recv.at[i, to], beside
        )

    def tell(k):
        return pltpu.make_async_remote_copy(
            src_ref=tally,
            dst_ref=counts.at[k],
            send_sem=count_send.at[k],
            recv_sem=count_recv.at[k],
            device_id={"dp": lax.rem(lax.axis_index("dp") + k, groups)},
            device_id_type=MESH,
        )

    def own_count():
        return pltpu.make_async_copy(tally, counts.at[0], count_sem)

    def own(i):
        return pltpu.make_async_copy(kv.at[i], blocks.at[i, 0], own_sem.at[i])

    def loads(i):
        slot = i % 2
        seq = i // kv_heads
        heads = pl.ds(pl.multiple_of(i % kv_heads * group, group), group)
        return [
            pltpu.make_async_copy(
                array.at[seq, :, heads], buf.at[slot], load_sem.at[slot, which]
            )
            for which, (array, buf) in enumerate(
                ((query, q_buf), (grad, g_buf), (output, o_buf))
            )
        ]

    def store(i):
        slot = i % 2
        seq = i // kv_heads
        heads = pl.ds(pl.multiple_of(i % kv_heads * group, group), group)
        return pltpu.make_async_copy(
            dq_buf.at[slot], query_grad.at[seq, :, heads], store_sem.at[slot]
        )

    def result(i):
        return pltpu.make_async_copy(parts.at[i, 0], kv_grad.at[i], out_sem.at[i])

    barrier = pltpu.get_barrier_semaphore()
    pl.semaphore_signal(barrier, inc=1, device_id={"seq": beside}, device_id_type=MESH)

    @pl.when(has_up)
    def _():
        pl.semaphore_signal(barrier, inc=1, device_id={"seq": above}, device_id_type=MESH)

    @pl.when(has_down)
    def _():
        pl.semaphore_signal(barrier, inc=1, device_id={"seq": below}, device_id_type=MESH)

    for k in range(1, groups):
        pl.semaphore_signal(
            barrier,
            inc=1,
            device_id={"dp": lax.rem(lax.axis_index("dp") + k, groups)},
            device_id_type=MESH,
        )

    own_count().start()

    def start_own(i, _):
        own(i).start()
        return 0

    lax.fori_loop(0, items, start_own, 0)
    for copy in loads(0):
        copy.start()

    peers = groups + has_up.astype(jnp.int32) + has_down.astype(jnp.int32)
    pl.semaphore_wait(barrier, peers)

    def start_sends(i):
        @pl.when(side == 0)
        def _():
            across(i, 0).start()

        @pl.when(has_up)
        def _():
            up(i, 0).start()

    start_sends(0)
    for k in range(1, groups):
        tell(k).start()

    @pl.when(level == 0)
    def _():
        start_sends(1)

    lane = lax.broadcasted_iota(jnp.int32, (count, dim), 1)
    wide[:, dim:] = jnp.where(lane < 3, 1.0, 0.0).astype(jnp.bfloat16)
    for r in range(1, slots):

        @pl.when(r > me)
        def _():
            def clear(i, _):
                blocks[i, r] = jnp.zeros(blocks.shape[2:], blocks.dtype)
                return 0

            lax.fori_loop(0, items, clear, 0)

    def detour(i):
        return (i % 2 == 1) | (i == 0)

    def climbs(i, r):
        if r == 1:
            return has_up & (side == 0) & jnp.logical_not(detour(i))
        if r == 3:
            return has_up & ((side == 0) | jnp.logical_not(detour(i)))
        return has_up

    def forward_first(i):
        arrived(i, 2)
        across(i, 2).start()

        @pl.when(has_up)
        def _():
            up(i, 2).start()

        if slots > 4:

            @pl.when(me >= 4)
            def _():
                arrived(i, 4)

                @pl.when(detour(i))
                def _():
                    across(i, 4).start()

                if slots > 6:

                    @pl.when(has_up)
                    def _():
                        up(i, 4).start()

    def forward_rest(i):
        for r in [1, 3] + list(range(5, slots)):

            @pl.when(me >= r)
            def _():
                arrived(i, r)
                if r + 2 < slots:

                    @pl.when(climbs(i, r))
                    def _():
                        up(i, r).start()

    def keys_of(i, start):
        return jnp.concatenate(
            [blocks[i, r, 0] for r in range(start // toks, (start + key_block) // toks)], axis=0
        )

    def compute(i):
        slot = i % 2
        seq = i // kv_heads
        length = lengths[seq]
        factor_live = (mean[0:1] * coef[seq])[None]
        base = me * toks
        for r in range(slots):
            wide[r * toks : (r + 1) * toks, :dim] = blocks[i, r, 1]
        key_acc[...] = jnp.zeros((count, dim), jnp.float32)
        value_acc[...] = jnp.zeros((count, dim), jnp.float32)

        def chunk(ch, _):
            tok0 = pl.multiple_of(ch * chunk_tokens, chunk_tokens)
            here = pl.ds(tok0, chunk_tokens)
            q_wide = q_buf[slot, here].astype(jnp.float32).reshape(rows, dim)
            q = q_wide.astype(jnp.bfloat16)
            position = (
                base + tok0 + lax.broadcasted_iota(jnp.int32, (chunk_tokens, group, dim), 0)
            )
            factor = jnp.where(position < length, factor_live, 0.0)
            g = (
                (g_buf[slot, here].astype(jnp.float32) * factor)
                .reshape(rows, dim)
                .astype(jnp.bfloat16)
            )
            g_f32 = g.astype(jnp.float32)
            o = o_buf[slot, here].astype(jnp.float32).reshape(rows, dim)
            delta = jnp.sum(g_f32 * o, axis=-1, keepdims=True)
            high = delta.astype(jnp.bfloat16).astype(jnp.float32)
            middle = (delta - high).astype(jnp.bfloat16).astype(jnp.float32)
            low = delta - high - middle
            row_lane = lax.broadcasted_iota(jnp.int32, (rows, dim), 1)
            extra = jnp.where(
                row_lane == 0,
                -high,
                jnp.where(row_lane == 1, -middle, jnp.where(row_lane == 2, -low, 0.0)),
            ).astype(jnp.bfloat16)
            g_wide = jnp.concatenate([g, extra], axis=1)

            top = jnp.full((8, rows), LOW, jnp.float32)
            for start in range(0, count, key_block):
                scores = dot(keys_of(i, start), q, NT)
                for r in range(start // toks, (start + key_block) // toks):
                    part = scores[r * toks - start : (r + 1) * toks - start]
                    if r == 0:
                        key_row = lax.broadcasted_iota(jnp.int32, (toks, rows), 0)
                        row_pos = (
                            tok0 + lax.broadcasted_iota(jnp.int32, (toks, rows), 1) // group
                        )
                        part = jnp.where(key_row <= row_pos, part, LOW)
                    s_ref[r * toks : (r + 1) * toks] = part
                    best = jnp.max(part.reshape(-1, 8, rows), axis=0)
                    if r:
                        best = jnp.where(r <= me, best, LOW)
                    top = jnp.maximum(top, best)
            top = jnp.max(top, axis=0, keepdims=True) * log2e

            total = jnp.zeros((8, rows), jnp.float32)
            for start in range(0, count, key_block):
                span = slice(start, start + key_block)
                dprob = dot(wide[span], g_wide, NT)
                for r in range(start // toks, (start + key_block) // toks):
                    here_keys = slice(r * toks, (r + 1) * toks)
                    shift = jnp.where(r <= me, top, -LOW) if r else top
                    e = jnp.exp2(s_ref[here_keys] * log2e - shift)
                    total = total + jnp.sum(e.reshape(-1, 8, rows), axis=0)
                    e_ref[here_keys] = e.astype(jnp.bfloat16)
                    ds_ref[here_keys] = (
                        e * dprob[r * toks - start : (r + 1) * toks - start]
                    ).astype(jnp.bfloat16)
            keys_all = jnp.concatenate([blocks[i, r, 0] for r in range(slots)], axis=0)
            acc = dot(keys_all, ds_ref[...], TN)
            inverse = 1.0 / jnp.sum(total, axis=0, keepdims=True)
            columns = jnp.broadcast_to(inverse, (dim, rows)).T
            dq = (acc * (inverse * scale)).T
            dq_buf[slot, here] = dq.reshape(chunk_tokens, group, dim).astype(dq_buf.dtype)
            q_low = (q_wide * columns).astype(jnp.bfloat16)
            g_low = (g_f32 * columns).astype(jnp.bfloat16)
            value_acc[...] += dot(e_ref[...], g_low)
            key_acc[...] += dot(ds_ref[...], q_low)
            return 0

        lax.fori_loop(0, toks // chunk_tokens, chunk, 0)
        for r in range(slots):
            span = slice(r * toks, (r + 1) * toks)
            parts[i, r, 0] = (key_acc[span] * scale).astype(parts.dtype)
            parts[i, r, 1] = value_acc[span].astype(parts.dtype)

    def add(i, r, extra):
        parts[i, r] = (parts[i, r].astype(jnp.float32) + extra.astype(jnp.float32)).astype(
            parts.dtype
        )

    def add_down(i, r):
        remote(
            parts.at[i, r], z_in.at[i, r], down_send.at[i, r], down_recv.at[i, r], beside
        ).wait_recv()
        add(i, r, z_in[i, r])

    def add_side(i, r, to):
        remote(
            parts.at[i, r], x_in.at[i, to], side_send.at[i, to], side_recv.at[i, to], beside
        ).wait_recv()
        add(i, r, x_in[i, to])

    def goes_aside(i, r):
        if r == 3:
            return (side == 1) | detour(i)
        return (side == 1) & detour(i)

    def reduce_first(i):
        for r in [3, 1, 5] + list(range(slots - 1, 5, -1)):
            if r >= slots:
                continue

            @pl.when(me >= r)
            def _():
                if r + 2 < slots:

                    @pl.when(climbs(i, r))
                    def _():
                        add_down(i, r)

                if r == 1:
                    sideways(i, r).start()
                elif r in (3, 5):
                    aside = goes_aside(i, r)

                    @pl.when(aside)
                    def _():
                        sideways(i, r).start()

                    @pl.when(jnp.logical_not(aside))
                    def _():
                        down(i, r).start()

                else:
                    down(i, r).start()

    def reduce_second(i):
        if slots > 4:

            @pl.when(me >= 4)
            def _():
                if slots > 6:

                    @pl.when(has_up)
                    def _():
                        add_down(i, 4)

                @pl.when(detour(i))
                def _():
                    add_side(i, 4, 2)

                down(i, 4).start()

        @pl.when(has_down)
        def _():
            @pl.when(has_up)
            def _():
                add_down(i, 2)

            add_side(i, 2, 1)
            down(i, 2).start()

        @pl.when(has_up)
        def _():
            add_down(i, 0)

        @pl.when(side == 0)
        def _():
            add_side(i, 0, 0)

        result(i).start()

    ahead = levels - 1 - level
    lag = 2 * ahead

    def step(u, _):
        t = u - (levels - 1)
        f = u - level

        @pl.when((f >= 0) & (f < items))
        def _():
            forward_rest(f)

        @pl.when((f >= -1) & (f < items - 1) & has_down)
        def _():
            forward_first(f + 1)

        @pl.when((f >= -1) & (f < items - 2))
        def _():
            start_sends(f + 2)

        @pl.when((t >= 0) & (t < items))
        def _():
            @pl.when(t == 0)
            def _():
                own_count().wait()
                for k in range(1, groups):
                    tell(k).wait_recv()
                sum_all = counts[0]
                for k in range(1, groups):
                    sum_all = sum_all + counts[k]
                mean[...] = sum_all.astype(jnp.float32) / (groups * lengths.shape[0])

            own(t).wait()
            for copy in loads(t):
                copy.wait()

            @pl.when(t + 1 < items)
            def _():
                for copy in loads(t + 1):
                    copy.start()

            @pl.when(t >= 2)
            def _():
                store(t - 2).wait()

            compute(t)
            store(t).start()

        @pl.when((t - lag >= 0) & (t - lag < items))
        def _():
            reduce_first(t - lag)

        @pl.when((t - lag - 1 >= 0) & (t - lag - 1 < items))
        def _():
            reduce_second(t - lag - 1)

        return 0

    lax.fori_loop(0, items + 3 * levels - 2, step, 0)

    for i in range(max(items - 2, 0), items):
        store(i).wait()
    for k in range(1, groups):
        tell(k).wait_send()

    def finish(i, _):
        result(i).wait()

        @pl.when(side == 0)
        def _():
            across(i, 0).wait_send()

        @pl.when(has_up)
        def _():
            up(i, 0).wait_send()

        for r in range(1, slots):

            @pl.when(me >= r)
            def _():
                if r == 2:
                    across(i, r).wait_send()
                if r == 4:

                    @pl.when(detour(i))
                    def _():
                        across(i, r).wait_send()

                if r + 2 < slots:

                    @pl.when(climbs(i, r))
                    def _():
                        up(i, r).wait_send()

                if r == 1:
                    sideways(i, r).wait_send()
                elif r in (3, 5):
                    aside = goes_aside(i, r)

                    @pl.when(aside)
                    def _():
                        sideways(i, r).wait_send()

                    @pl.when(jnp.logical_not(aside))
                    def _():
                        down(i, r).wait_send()

                else:
                    down(i, r).wait_send()

        return 0

    lax.fori_loop(0, items, finish, 0)


def fused(lengths, coef, tally, query, grad, output, kv, slots, groups):
    items, _, toks, dim = kv.shape
    seqs, _, heads, _ = query.shape
    group = heads * seqs // items
    count = slots * toks
    chunk_tokens = min(CHUNK_TOKENS, toks)
    rows = chunk_tokens * group
    key_block = max(toks, min(KEY_BLOCK, count))
    bf16 = jnp.bfloat16
    block = (2, toks, dim)
    dma = pltpu.SemaphoreType.DMA
    anywhere = pl.BlockSpec(memory_space=pl.ANY)
    smem = pl.BlockSpec(memory_space=pltpu.SMEM)
    return pl.pallas_call(
        functools.partial(
            fused_kernel,
            scale=1.0 / math.sqrt(dim),
            chunk_tokens=chunk_tokens,
            key_block=key_block,
        ),
        out_shape=(
            jax.ShapeDtypeStruct(query.shape, bf16),
            jax.ShapeDtypeStruct(kv.shape, bf16),
        ),
        in_specs=[smem] * 2 + [anywhere] * 5,
        out_specs=(anywhere,) * 2,
        scratch_shapes=[
            pltpu.VMEM((items, slots) + block, bf16),
            pltpu.VMEM((items, slots) + block, bf16),
            pltpu.VMEM((items, slots - 2) + block, bf16),
            pltpu.VMEM((items, 3) + block, bf16),
            pltpu.VMEM((2, toks, group, dim), bf16),
            pltpu.VMEM((2, toks, group, dim), bf16),
            pltpu.VMEM((2, toks, group, dim), bf16),
            pltpu.VMEM((2, toks, group, dim), bf16),
            pltpu.VMEM((count, rows), jnp.float32),
            pltpu.VMEM((count, rows), bf16),
            pltpu.VMEM((count, rows), bf16),
            pltpu.VMEM((count, dim), jnp.float32),
            pltpu.VMEM((count, dim), jnp.float32),
            pltpu.VMEM((count, 2 * dim), bf16),
            pltpu.VMEM((groups,) + tally.shape, jnp.int32),
            pltpu.VMEM(tally.shape, jnp.float32),
            dma((items,)),
            dma((2, 3)),
            dma((2,)),
            dma((items, slots)),
            dma((items, 3)),
            dma((items, slots)),
            dma((items, slots)),
            dma((items, 3)),
            dma((items, slots)),
            dma((items, 3)),
            dma((items,)),
            dma,
            dma((groups,)),
            dma((groups,)),
        ],
        compiler_params=pltpu.CompilerParams(
            collective_id=0,
            has_side_effects=True,
            vmem_limit_bytes=62 * 1024 * 1024,
        ),
    )(lengths, coef, tally, query, grad, output, kv)


def body(query, keys, values, output, out_grad, lengths, margins):
    slots = lax.axis_size("seq")
    seqs, toks, heads, dim = query.shape
    kv_heads = keys.shape[2]
    kv = jnp.stack([keys, values], axis=1).transpose(0, 3, 1, 2, 4)
    kv = kv.reshape(seqs * kv_heads, 2, toks, dim)
    tally = jnp.full((8, dim), jnp.sum(lengths), jnp.int32)
    weight = jax.nn.sigmoid(-margins)
    signs = jnp.tile(jnp.array([-1.0, 1.0], jnp.float32), margins.shape[0])
    coef = jnp.repeat(weight, 2) * signs * 4.0 / lengths.astype(jnp.float32)
    query_grad, grads = fused(
        lengths, coef, tally, query, out_grad, output, kv, slots, lax.axis_size("dp")
    )
    grads = grads.reshape(seqs, kv_heads, 2, toks, dim)
    key_grad = grads[:, :, 0].transpose(0, 2, 1, 3)
    value_grad = grads[:, :, 1].transpose(0, 2, 1, 3)
    return (query_grad, key_grad, value_grad)


def solution(mesh):
    tokens = P("dp", "seq", None, None)
    return jax.shard_map(
        body,
        mesh=mesh,
        in_specs=(tokens,) * 5 + (P("dp"), P("dp")),
        out_specs=(tokens,) * 3,
        check_vma=False,
    )
```

```python
import functools
import math

import jax
import jax.numpy as jnp
from jax import lax
from jax.experimental import pallas as pl
from jax.experimental.pallas import tpu as pltpu
from jax.sharding import PartitionSpec as P

CHUNK_TOKENS = 128
KEY_BLOCK = 1024
LOW = -1e30
MESH = pl.DeviceIdType.MESH
NT = (((1,), (1,)), ((), ()))
TN = (((0,), (0,)), ((), ()))


def dot(a, b, dims=(((1,), (0,)), ((), ()))):
    return lax.dot_general(a, b, dims, preferred_element_type=jnp.float32)


def fused_kernel(
    lengths,
    coef,
    tally,
    query,
    grad,
    output,
    kv,
    query_grad,
    kv_grad,
    blocks,
    parts,
    z_in,
    x_in,
    q_buf,
    g_buf,
    o_buf,
    dq_buf,
    s_ref,
    e_ref,
    ds_ref,
    key_acc,
    value_acc,
    wide,
    counts,
    mean,
    own_sem,
    load_sem,
    store_sem,
    up_send,
    across_send,
    block_recv,
    down_send,
    side_send,
    down_recv,
    side_recv,
    out_sem,
    count_sem,
    count_send,
    count_recv,
    *,
    scale,
    chunk_tokens,
    key_block,
):
    items, slots, _, toks, dim = blocks.shape
    group = q_buf.shape[2]
    kv_heads = items // query.shape[0]
    levels = slots // 2
    rows = chunk_tokens * group
    count = slots * toks
    log2e = scale * math.log2(math.e)

    groups = counts.shape[0]
    me = lax.axis_index("seq")
    level = me // 2
    side = me % 2
    has_up = level < levels - 1
    has_down = level >= 1
    above = jnp.minimum(me + 2, slots - 1)
    below = jnp.maximum(me - 2, 0)
    beside = me + 1 - 2 * side

    def remote(src, dst, send, recv, place):
        return pltpu.make_async_remote_copy(
            src_ref=src,
            dst_ref=dst,
            send_sem=send,
            recv_sem=recv,
            device_id={"seq": place},
            device_id_type=MESH,
        )

    def up(i, r):
        src = kv.at[i] if r == 0 else blocks.at[i, r]
        return remote(src, blocks.at[i, r + 2], up_send.at[i, r], block_recv.at[i, r + 2], above)

    def across(i, r):
        to = r + 1 - 2 * side if r else 1
        src = kv.at[i] if r == 0 else blocks.at[i, r]
        return remote(
            src, blocks.at[i, to], across_send.at[i, r // 2], block_recv.at[i, to], beside
        )

    def arrived(i, r):
        remote(
            blocks.at[i, r], blocks.at[i, r], up_send.at[i, r], block_recv.at[i, r], beside
        ).wait_recv()

    def down(i, r):
        return remote(
            parts.at[i, r], z_in.at[i, r - 2], down_send.at[i, r], down_recv.at[i, r - 2], below
        )

    def sideways(i, r):
        to = 1 - side if r == 1 else (2 - side if r == 3 else 2)
        return remote(
            parts.at[i, r], x_in.at[i, to], side_send.at[i, r // 2], side_recv.at[i, to], beside
        )

    def tell(k):
        return pltpu.make_async_remote_copy(
            src_ref=tally,
            dst_ref=counts.at[k],
            send_sem=count_send.at[k],
            recv_sem=count_recv.at[k],
            device_id={"dp": lax.rem(lax.axis_index("dp") + k, groups)},
            device_id_type=MESH,
        )

    def own_count():
        return pltpu.make_async_copy(tally, counts.at[0], count_sem)

    def own(i):
        return pltpu.make_async_copy(kv.at[i], blocks.at[i, 0], own_sem.at[i])

    def loads(i):
        slot = i % 2
        seq = i // kv_heads
        heads = pl.ds(pl.multiple_of(i % kv_heads * group, group), group)
        return [
            pltpu.make_async_copy(
                array.at[seq, :, heads], buf.at[slot], load_sem.at[slot, which]
            )
            for which, (array, buf) in enumerate(
                ((query, q_buf), (grad, g_buf), (output, o_buf))
            )
        ]

    def store(i):
        slot = i % 2
        seq = i // kv_heads
        heads = pl.ds(pl.multiple_of(i % kv_heads * group, group), group)
        return pltpu.make_async_copy(
            dq_buf.at[slot], query_grad.at[seq, :, heads], store_sem.at[slot]
        )

    def result(i):
        return pltpu.make_async_copy(parts.at[i, 0], kv_grad.at[i], out_sem.at[i])

    barrier = pltpu.get_barrier_semaphore()
    pl.semaphore_signal(barrier, inc=1, device_id={"seq": beside}, device_id_type=MESH)

    @pl.when(has_up)
    def _():
        pl.semaphore_signal(barrier, inc=1, device_id={"seq": above}, device_id_type=MESH)

    @pl.when(has_down)
    def _():
        pl.semaphore_signal(barrier, inc=1, device_id={"seq": below}, device_id_type=MESH)

    for k in range(1, groups):
        pl.semaphore_signal(
            barrier,
            inc=1,
            device_id={"dp": lax.rem(lax.axis_index("dp") + k, groups)},
            device_id_type=MESH,
        )

    own_count().start()

    def start_own(i, _):
        own(i).start()
        return 0

    lax.fori_loop(0, items, start_own, 0)
    for copy in loads(0):
        copy.start()

    peers = groups + has_up.astype(jnp.int32) + has_down.astype(jnp.int32)
    pl.semaphore_wait(barrier, peers)

    def start_sends(i):
        @pl.when(side == 0)
        def _():
            across(i, 0).start()

        @pl.when(has_up)
        def _():
            up(i, 0).start()

    start_sends(0)
    for k in range(1, groups):
        tell(k).start()

    @pl.when(level == 0)
    def _():
        start_sends(1)

    lane = lax.broadcasted_iota(jnp.int32, (count, dim), 1)
    wide[:, dim:] = jnp.where(lane < 3, 1.0, 0.0).astype(jnp.bfloat16)
    for r in range(1, slots):

        @pl.when(r > me)
        def _():
            def clear(i, _):
                blocks[i, r] = jnp.zeros(blocks.shape[2:], blocks.dtype)
                return 0

            lax.fori_loop(0, items, clear, 0)

    def detour(i):
        return (i % 2 == 1) | (i == 0)

    def climbs(i, r):
        if r == 1:
            return has_up & (side == 0) & jnp.logical_not(detour(i))
        if r == 3:
            return has_up & ((side == 0) | jnp.logical_not(detour(i)))
        return has_up

    def forward_first(i):
        arrived(i, 2)
        across(i, 2).start()

        @pl.when(has_up)
        def _():
            up(i, 2).start()

        if slots > 4:

            @pl.when(me >= 4)
            def _():
                arrived(i, 4)

                @pl.when(detour(i))
                def _():
                    across(i, 4).start()

                if slots > 6:

                    @pl.when(has_up)
                    def _():
                        up(i, 4).start()

    def forward_rest(i):
        for r in [1, 3] + list(range(5, slots)):

            @pl.when(me >= r)
            def _():
                arrived(i, r)
                if r + 2 < slots:

                    @pl.when(climbs(i, r))
                    def _():
                        up(i, r).start()

    def keys_of(i, start):
        return jnp.concatenate(
            [blocks[i, r, 0] for r in range(start // toks, (start + key_block) // toks)], axis=0
        )

    def compute(i):
        slot = i % 2
        seq = i // kv_heads
        length = lengths[seq]
        factor_live = (mean[0:1] * coef[seq])[None]
        base = me * toks
        for r in range(slots):
            wide[r * toks : (r + 1) * toks, :dim] = blocks[i, r, 1]

        chunks = toks // chunk_tokens

        def chunk(ch):
            tok0 = ch * chunk_tokens
            here = pl.ds(tok0, chunk_tokens)
            q_wide = q_buf[slot, here].astype(jnp.float32).reshape(rows, dim)
            q = q_wide.astype(jnp.bfloat16)
            position = (
                base + tok0 + lax.broadcasted_iota(jnp.int32, (chunk_tokens, group, dim), 0)
            )
            factor = jnp.where(position < length, factor_live, 0.0)
            g = (
                (g_buf[slot, here].astype(jnp.float32) * factor)
                .reshape(rows, dim)
                .astype(jnp.bfloat16)
            )
            g_f32 = g.astype(jnp.float32)
            o = o_buf[slot, here].astype(jnp.float32).reshape(rows, dim)
            delta = jnp.sum(g_f32 * o, axis=-1, keepdims=True)
            high = delta.astype(jnp.bfloat16).astype(jnp.float32)
            middle = (delta - high).astype(jnp.bfloat16).astype(jnp.float32)
            low = delta - high - middle
            row_lane = lax.broadcasted_iota(jnp.int32, (rows, dim), 1)
            extra = jnp.where(
                row_lane == 0,
                -high,
                jnp.where(row_lane == 1, -middle, jnp.where(row_lane == 2, -low, 0.0)),
            ).astype(jnp.bfloat16)
            g_wide = jnp.concatenate([g, extra], axis=1)

            top = jnp.full((8, rows), LOW, jnp.float32)
            for start in range(0, count, key_block):
                scores = dot(keys_of(i, start), q, NT)
                for r in range(start // toks, (start + key_block) // toks):
                    part = scores[r * toks - start : (r + 1) * toks - start]
                    if r == 0:
                        key_row = lax.broadcasted_iota(jnp.int32, (toks, rows), 0)
                        row_pos = (
                            tok0 + lax.broadcasted_iota(jnp.int32, (toks, rows), 1) // group
                        )
                        part = jnp.where(key_row <= row_pos, part, LOW)
                    s_ref[r * toks : (r + 1) * toks] = part
                    best = jnp.max(part.reshape(-1, 8, rows), axis=0)
                    if r:
                        best = jnp.where(r <= me, best, LOW)
                    top = jnp.maximum(top, best)
            top = jnp.max(top, axis=0, keepdims=True) * log2e

            total = jnp.zeros((8, rows), jnp.float32)
            for start in range(0, count, key_block):
                span = slice(start, start + key_block)
                dprob = dot(wide[span], g_wide, NT)
                for r in range(start // toks, (start + key_block) // toks):
                    here_keys = slice(r * toks, (r + 1) * toks)
                    shift = jnp.where(r <= me, top, -LOW) if r else top
                    e = jnp.exp2(s_ref[here_keys] * log2e - shift)
                    total = total + jnp.sum(e.reshape(-1, 8, rows), axis=0)
                    e_ref[here_keys] = e.astype(jnp.bfloat16)
                    ds_ref[here_keys] = (
                        e * dprob[r * toks - start : (r + 1) * toks - start]
                    ).astype(jnp.bfloat16)
            keys_all = jnp.concatenate([blocks[i, r, 0] for r in range(slots)], axis=0)
            acc = dot(keys_all, ds_ref[...], TN)
            inverse = 1.0 / jnp.sum(total, axis=0, keepdims=True)
            columns = jnp.broadcast_to(inverse, (dim, rows)).T
            dq = (acc * (inverse * scale)).T
            dq_buf[slot, here] = dq.reshape(chunk_tokens, group, dim).astype(dq_buf.dtype)
            q_low = (q_wide * columns).astype(jnp.bfloat16)
            g_low = (g_f32 * columns).astype(jnp.bfloat16)
            value_sum = dot(e_ref[...], g_low)
            if ch:
                value_sum = value_acc[...] + value_sum
            if ch < chunks - 1:
                value_acc[...] = value_sum
            else:
                for r in range(slots):
                    parts[i, r, 1] = value_sum[r * toks : (r + 1) * toks].astype(parts.dtype)
            key_sum = dot(ds_ref[...], q_low)
            if ch:
                key_sum = key_acc[...] + key_sum
            if ch < chunks - 1:
                key_acc[...] = key_sum
            else:
                for r in range(slots):
                    span = slice(r * toks, (r + 1) * toks)
                    parts[i, r, 0] = (key_sum[span] * scale).astype(parts.dtype)

        for ch in range(chunks):
            chunk(ch)

    def add(i, r, extra):
        parts[i, r] = (parts[i, r].astype(jnp.float32) + extra.astype(jnp.float32)).astype(
            parts.dtype
        )

    def add_down(i, r):
        remote(
            parts.at[i, r], z_in.at[i, r], down_send.at[i, r], down_recv.at[i, r], beside
        ).wait_recv()
        add(i, r, z_in[i, r])

    def add_side(i, r, to):
        remote(
            parts.at[i, r], x_in.at[i, to], side_send.at[i, to], side_recv.at[i, to], beside
        ).wait_recv()
        add(i, r, x_in[i, to])

    def goes_aside(i, r):
        if r == 3:
            return (side == 1) | detour(i)
        return (side == 1) & detour(i)

    def reduce_first(i):
        for r in [3, 1, 5] + list(range(slots - 1, 5, -1)):
            if r >= slots:
                continue

            @pl.when(me >= r)
            def _():
                if r + 2 < slots:

                    @pl.when(climbs(i, r))
                    def _():
                        add_down(i, r)

                if r == 1:
                    sideways(i, r).start()
                elif r in (3, 5):
                    aside = goes_aside(i, r)

                    @pl.when(aside)
                    def _():
                        sideways(i, r).start()

                    @pl.when(jnp.logical_not(aside))
                    def _():
                        down(i, r).start()

                else:
                    down(i, r).start()

    def reduce_second(i):
        if slots > 4:

            @pl.when(me >= 4)
            def _():
                if slots > 6:

                    @pl.when(has_up)
                    def _():
                        add_down(i, 4)

                @pl.when(detour(i))
                def _():
                    add_side(i, 4, 2)

                down(i, 4).start()

        @pl.when(has_down)
        def _():
            @pl.when(has_up)
            def _():
                add_down(i, 2)

            add_side(i, 2, 1)
            down(i, 2).start()

        @pl.when(has_up)
        def _():
            add_down(i, 0)

        @pl.when(side == 0)
        def _():
            add_side(i, 0, 0)

        result(i).start()

    ahead = levels - 1 - level
    lag = ahead + jnp.minimum(ahead, 1)

    def step(u, _):
        t = u - (levels - 1)
        f = u - level

        @pl.when((f >= 0) & (f < items))
        def _():
            forward_rest(f)

        @pl.when((f >= -1) & (f < items - 1) & has_down)
        def _():
            forward_first(f + 1)

        @pl.when((f >= -1) & (f < items - 2))
        def _():
            start_sends(f + 2)

        @pl.when((t >= 0) & (t < items))
        def _():
            @pl.when(t == 0)
            def _():
                own_count().wait()
                for k in range(1, groups):
                    tell(k).wait_recv()
                sum_all = counts[0]
                for k in range(1, groups):
                    sum_all = sum_all + counts[k]
                mean[...] = sum_all.astype(jnp.float32) / (groups * lengths.shape[0])

            own(t).wait()
            for copy in loads(t):
                copy.wait()

            @pl.when(t + 1 < items)
            def _():
                for copy in loads(t + 1):
                    copy.start()

            @pl.when(t >= 2)
            def _():
                store(t - 2).wait()

            compute(t)
            store(t).start()

        @pl.when((t - lag >= 0) & (t - lag < items))
        def _():
            reduce_first(t - lag)

        @pl.when((t - lag - 1 >= 0) & (t - lag - 1 < items))
        def _():
            reduce_second(t - lag - 1)

        return 0

    lax.fori_loop(0, items + 2 * levels, step, 0)

    for i in range(max(items - 2, 0), items):
        store(i).wait()
    for k in range(1, groups):
        tell(k).wait_send()

    def finish(i, _):
        result(i).wait()

        @pl.when(side == 0)
        def _():
            across(i, 0).wait_send()

        @pl.when(has_up)
        def _():
            up(i, 0).wait_send()

        for r in range(1, slots):

            @pl.when(me >= r)
            def _():
                if r == 2:
                    across(i, r).wait_send()
                if r == 4:

                    @pl.when(detour(i))
                    def _():
                        across(i, r).wait_send()

                if r + 2 < slots:

                    @pl.when(climbs(i, r))
                    def _():
                        up(i, r).wait_send()

                if r == 1:
                    sideways(i, r).wait_send()
                elif r in (3, 5):
                    aside = goes_aside(i, r)

                    @pl.when(aside)
                    def _():
                        sideways(i, r).wait_send()

                    @pl.when(jnp.logical_not(aside))
                    def _():
                        down(i, r).wait_send()

                else:
                    down(i, r).wait_send()

        return 0

    lax.fori_loop(0, items, finish, 0)


def fused(lengths, coef, tally, query, grad, output, kv, slots, groups):
    items, _, toks, dim = kv.shape
    seqs, _, heads, _ = query.shape
    group = heads * seqs // items
    count = slots * toks
    chunk_tokens = min(CHUNK_TOKENS, toks)
    rows = chunk_tokens * group
    key_block = max(toks, min(KEY_BLOCK, count))
    bf16 = jnp.bfloat16
    block = (2, toks, dim)
    dma = pltpu.SemaphoreType.DMA
    anywhere = pl.BlockSpec(memory_space=pl.ANY)
    smem = pl.BlockSpec(memory_space=pltpu.SMEM)
    return pl.pallas_call(
        functools.partial(
            fused_kernel,
            scale=1.0 / math.sqrt(dim),
            chunk_tokens=chunk_tokens,
            key_block=key_block,
        ),
        out_shape=(
            jax.ShapeDtypeStruct(query.shape, bf16),
            jax.ShapeDtypeStruct(kv.shape, bf16),
        ),
        in_specs=[smem] * 2 + [anywhere] * 5,
        out_specs=(anywhere,) * 2,
        scratch_shapes=[
            pltpu.VMEM((items, slots) + block, bf16),
            pltpu.VMEM((items, slots) + block, bf16),
            pltpu.VMEM((items, slots - 2) + block, bf16),
            pltpu.VMEM((items, 3) + block, bf16),
            pltpu.VMEM((2, toks, group, dim), bf16),
            pltpu.VMEM((2, toks, group, dim), bf16),
            pltpu.VMEM((2, toks, group, dim), bf16),
            pltpu.VMEM((2, toks, group, dim), bf16),
            pltpu.VMEM((count, rows), jnp.float32),
            pltpu.VMEM((count, rows), bf16),
            pltpu.VMEM((count, rows), bf16),
            pltpu.VMEM((count, dim), jnp.float32),
            pltpu.VMEM((count, dim), jnp.float32),
            pltpu.VMEM((count, 2 * dim), bf16),
            pltpu.VMEM((groups,) + tally.shape, jnp.int32),
            pltpu.VMEM(tally.shape, jnp.float32),
            dma((items,)),
            dma((2, 3)),
            dma((2,)),
            dma((items, slots)),
            dma((items, 3)),
            dma((items, slots)),
            dma((items, slots)),
            dma((items, 3)),
            dma((items, slots)),
            dma((items, 3)),
            dma((items,)),
            dma,
            dma((groups,)),
            dma((groups,)),
        ],
        compiler_params=pltpu.CompilerParams(
            collective_id=0,
            has_side_effects=True,
            vmem_limit_bytes=62 * 1024 * 1024,
        ),
    )(lengths, coef, tally, query, grad, output, kv)


def body(query, keys, values, output, out_grad, lengths, margins):
    slots = lax.axis_size("seq")
    seqs, toks, heads, dim = query.shape
    kv_heads = keys.shape[2]
    kv = jnp.stack([keys, values], axis=1).transpose(0, 3, 1, 2, 4)
    kv = kv.reshape(seqs * kv_heads, 2, toks, dim)
    tally = jnp.full((8, dim), jnp.sum(lengths), jnp.int32)
    weight = jax.nn.sigmoid(-margins)
    signs = jnp.tile(jnp.array([-1.0, 1.0], jnp.float32), margins.shape[0])
    coef = jnp.repeat(weight, 2) * signs * 4.0 / lengths.astype(jnp.float32)
    query_grad, grads = fused(
        lengths, coef, tally, query, out_grad, output, kv, slots, lax.axis_size("dp")
    )
    grads = grads.reshape(seqs, kv_heads, 2, toks, dim)
    key_grad = grads[:, :, 0].transpose(0, 2, 1, 3)
    value_grad = grads[:, :, 1].transpose(0, 2, 1, 3)
    return (query_grad, key_grad, value_grad)


def solution(mesh):
    tokens = P("dp", "seq", None, None)
    return jax.shard_map(
        body,
        mesh=mesh,
        in_specs=(tokens,) * 5 + (P("dp"), P("dp")),
        out_specs=(tokens,) * 3,
        check_vma=False,
    )
```
